32 devices in a mesh: lat: 4 (over y, core), lon: 8 (over z, x).
Axes of the slice: x: 2, y: 2, z: 4, core: 2. Of those that a mesh axis runs over, the one named last changes fastest.
Arguments:
- control: bfloat16 [80, 32, 64, 512], P(None, None, 'lon', 'lat'), may hold values from -6 to 6
- ensemble: bfloat16 [80, 32, 64, 512], P(None, None, 'lon', 'lat'), may hold values from -1.1953125 to 1.1953125
- level_mix: bfloat16 [32, 32], replicated, may hold values from -1 to 1
- lat_taps: float32 [4], replicated, may hold values from 0.1 to 0.6
- lon_taps: float32 [4], replicated, may hold values from 0.1 to 0.6
- obs_location: int32 [8, 4, 2048], P('lon', 'lat'), may hold values from 0 to 32767
- obs_count: int32 [8, 4], P('lon', 'lat'), may hold values from 512 to 2048, as said below
- obs_keep: int32 [8, 4, 2048], P('lon', 'lat'), may hold values 0 or 1
- innovation: float32 [8, 4, 2048], P('lon', 'lat'), may hold values from -6 to 6
- obs_weight: float32 [8, 4, 2048], P('lon', 'lat'), may hold values from 0.25 to 4
Outputs:
- gradient: float32 [80, 32, 64, 512], P(None, None, 'lon', 'lat')
- upper_factor: float32 [80, 80], replicated
The draws below stay inside these ranges and needn't reach their ends.
Inputs may be any that keep to these rules, and one draw needn't show every extreme that they name: `obs_count`: live slots of a tile come first; some tile has all 2048 slots live.
All inputs are finite; a program needn't handle non-finite values. No bound on the sum of `obs_keep` on one device may be relied on, other than what follows from the above.
Results may differ from the reference program's by a relative error of at most 0.0028.
Values may be sent and summed in bfloat16 or wider, within the bound.
A program may use at most 128 MiB of HBM per device.

```python
import math
import jax
import jax.numpy as jnp
from jax import lax

MEMBERS = 80
LEVELS = 32
LON_DEV = 8
LAT_DEV = 128
OBS_DEV = 2048
TILES_LON = 8
TILES_LAT = 4
NLON = 64
NLAT = 512
OBS_ALL = 65536


def draw_obs_count(key, part):
    lon_index = jnp.arange(TILES_LON, dtype=jnp.int32)[:, None]
    lat_index = jnp.arange(TILES_LAT, dtype=jnp.int32)[None, :]
    span_all = max(TILES_LON + TILES_LAT - 2, 1)
    quarter = OBS_DEV // 4
    rising = (OBS_DEV - quarter) * (lon_index + lat_index) // span_all
    jitter = jax.random.randint(key, (TILES_LON, TILES_LAT), 0, OBS_DEV // 8 + 1, dtype=jnp.int32)
    return jnp.minimum(quarter + rising + jitter, OBS_DEV).astype(jnp.int32)


def touch_ends(entries, key, least, high):
    shape = entries.shape
    spot = [jax.random.randint(jax.random.fold_in(key, axis), (), 0, shape[axis]) for axis in range(len(shape))]
    entries = entries.at[tuple(spot)].set(least)
    longest = shape.index(max(shape))
    spot[longest] = (spot[longest] + 1) % shape[longest]
    return entries.at[tuple(spot)].set(high)


def levels(own_key, shape, pieces, least, high):
    factor_of, own = 1.0, jax.random.fold_in(own_key, 6)
    for dim, parts in pieces:
        steps = jnp.exp(jax.random.uniform(jax.random.fold_in(own, dim), (parts,), jnp.float32, least / len(pieces), high / len(pieces)))
        factor_of = factor_of * jnp.repeat(steps, shape[dim] // parts).reshape([-1 if axis == dim else 1 for axis in range(len(shape))])
    return factor_of


def centred(key, shape, scale, bound, pieces=(), kind=jnp.bfloat16):
    drawn = jax.random.normal(key, shape, jnp.float32) * scale
    if len(pieces) > 0:
        drawn = levels(key, shape, pieces, -0.22, 0.18) * drawn
    return jnp.clip(drawn, min=-bound, max=bound).astype(kind)


def setup_inputs(seed: int = 0) -> dict:
    key_list = jax.random.split(jax.random.key(seed), 11)
    control = centred(key_list[0], (MEMBERS, LEVELS, NLON, NLAT), 1.0, 6.0, ((2, 8), (3, 4)))
    ensemble = centred(key_list[1], (MEMBERS, LEVELS, NLON, NLAT), 0.2, 1.1953125, ((2, 8), (3, 4)))
    level_mix = centred(key_list[2], (LEVELS, LEVELS), LEVELS ** -0.5, 1.0)
    lat_taps = jnp.clip(jnp.exp(jax.random.uniform(key_list[3], (4,), jnp.float32, math.log(0.1), math.log(0.6))), 0.1, 0.6)
    lon_taps = jnp.clip(jnp.exp(jax.random.uniform(key_list[4], (4,), jnp.float32, math.log(0.1), math.log(0.6))), 0.1, 0.6)
    obs_location = touch_ends(jax.random.randint(key_list[5], (TILES_LON, TILES_LAT, OBS_DEV), 0, LEVELS * LON_DEV * LAT_DEV), jax.random.fold_in(key_list[5], 1), 0, (LEVELS * LON_DEV * LAT_DEV) - 1).astype(jnp.int32)
    obs_count = draw_obs_count(jax.random.fold_in(key_list[10], 71), 0)
    obs_keep = touch_ends((jax.random.randint(key_list[7], (TILES_LON, TILES_LAT, OBS_DEV), 0, 8) < 7).astype(jnp.int32), jax.random.fold_in(key_list[7], 1), 0, 1)
    innovation = centred(key_list[8], (TILES_LON, TILES_LAT, OBS_DEV), 1.0, 6.0, ((0, 8), (1, 4)), jnp.float32)
    obs_weight = jnp.clip(jnp.exp(math.log(4.0) - 2.7725887 * jax.random.uniform(key_list[9], (TILES_LON, TILES_LAT, OBS_DEV), jnp.float32) ** levels(key_list[9], (TILES_LON, TILES_LAT, OBS_DEV), ((0, 8), (1, 4)), -0.2, 0.2)), 0.25, 4.0)
    return {"control": control, "ensemble": ensemble, "level_mix": level_mix, "lat_taps": lat_taps, "lon_taps": lon_taps, "obs_location": obs_location, "obs_count": obs_count, "obs_keep": obs_keep, "innovation": innovation, "obs_weight": obs_weight}


OFFSETS = (-2, -1, 1, 2)

def shifted_sum(field, weights, dimension, direction, periodic):
    extent = field.shape[dimension]
    summed = field
    widths = [(0, 0)] * field.ndim
    widths[dimension] = (2, 2)
    padded = jnp.pad(field, widths)
    for position in range(4):
        shift = direction * OFFSETS[position]
        if periodic:
            moved = jnp.roll(field, -shift, axis=dimension)
        else:
            moved = lax.slice_in_dim(padded, 2 + shift, 2 + shift + extent, axis=dimension)
        summed = summed + weights[position] * moved
    return summed

def reference(control, ensemble, level_mix, lat_taps, lon_taps, obs_location, obs_count, obs_keep, innovation, obs_weight):

    def forward_member(carried, paired):
        control_m, ensemble_m = paired
        mixed_m = jnp.dot(level_mix.astype(jnp.float32), control_m.reshape(LEVELS, -1).astype(jnp.float32), preferred_element_type=jnp.float32).astype(jnp.bfloat16)
        mixed_f = lax.optimization_barrier(mixed_m).astype(jnp.float32).reshape(LEVELS, NLON, NLAT)
        rowpass = shifted_sum(mixed_f, lat_taps, 2, 1, False)
        localized = shifted_sum(rowpass, lon_taps, 1, 1, True)
        return (carried + ensemble_m.astype(jnp.float32) * localized, None)
    increment, unused = lax.scan(forward_member, jnp.zeros((LEVELS, NLON, NLAT), jnp.float32), (control, ensemble))
    tile_lon = jnp.arange(TILES_LON, dtype=jnp.int32)[:, None, None]
    tile_lat = jnp.arange(TILES_LAT, dtype=jnp.int32)[None, :, None]
    level_of = obs_location // (LON_DEV * LAT_DEV)
    column_of = tile_lon * LON_DEV + obs_location // LAT_DEV % LON_DEV
    row_of = tile_lat * LAT_DEV + obs_location % LAT_DEV
    flat_index = ((level_of * NLON + column_of) * NLAT + row_of).astype(jnp.int32).reshape(-1)
    slot_ids = jnp.arange(OBS_DEV, dtype=jnp.int32)[None, None, :]
    live_slots = (slot_ids < obs_count[:, :, None]).astype(jnp.float32) * obs_keep.astype(jnp.float32)
    weights = (live_slots * obs_weight).reshape(-1)
    misfit = weights * (increment.reshape(-1)[flat_index] - innovation.reshape(-1))
    pulled = jnp.zeros((LEVELS * NLON * NLAT,), jnp.float32).at[flat_index].add(misfit).reshape(LEVELS, NLON, NLAT)

    def adjoint_member(paired):
        control_m, ensemble_m = paired
        pulled_m = (ensemble_m.astype(jnp.float32) * pulled).astype(jnp.bfloat16)
        pulled_f = lax.optimization_barrier(pulled_m).astype(jnp.float32)
        colpass = shifted_sum(pulled_f, lon_taps, 1, -1, True)
        spread = shifted_sum(colpass, lat_taps, 2, -1, False).astype(jnp.bfloat16)
        mixed_back = jnp.dot(level_mix.T.astype(jnp.float32), spread.reshape(LEVELS, -1).astype(jnp.float32), preferred_element_type=jnp.float32)
        return control_m.astype(jnp.float32) + mixed_back.reshape(LEVELS, NLON, NLAT)
    gradient = lax.map(adjoint_member, (control, ensemble))
    columns = ensemble.reshape(MEMBERS, -1)[:, flat_index]
    anomaly = columns.astype(jnp.float32) * jnp.sqrt(weights)[None, :]
    gram = jnp.dot(anomaly, anomaly.T, precision=lax.Precision.HIGHEST)
    identity = jnp.eye(MEMBERS, dtype=jnp.float32)
    system = identity + MEMBERS / OBS_ALL * gram
    upper_factor = jnp.linalg.cholesky(system).T
    return (gradient, upper_factor)
```

```python
import jax
import jax.numpy as jnp
from jax import lax
from jax.experimental import pallas as pl
from jax.experimental.pallas import tpu as pltpu
from jax.sharding import PartitionSpec as P

OFFSETS = (-2, -1, 1, 2)
F32, BF = jnp.float32, jnp.bfloat16
VMEM_LIMIT = 56 * 1024 * 1024


def split2(x):
    hi = lax.reduce_precision(x, 8, 7)
    return hi.astype(BF), (x - hi).astype(BF)


def tap_of(diff, taps):
    out = (diff == 0).astype(F32)
    for t in range(4):
        out = out + jnp.where(diff == OFFSETS[t], taps[t], 0.0)
    return out


def nn(a, b):
    return jnp.dot(a, b, preferred_element_type=F32)


def nt(a, b):
    return lax.dot_general(a, b, (((1,), (1,)), ((), ())), preferred_element_type=F32)


def tn(a, b):
    return lax.dot_general(a, b, (((0,), (0,)), ((), ())), preferred_element_type=F32)


def part3(x):
    a = x.astype(BF)
    r = x - a.astype(F32)
    b = r.astype(BF)
    c = (r - b.astype(F32)).astype(BF)
    return a, b, c


def edge_kernel(c_ref, e_ref, sel_ref, perm_ref, ce_ref, ee_ref, lo_ref, hi_ref):
    half = lo_ref.shape[1]
    for m in range(c_ref.shape[0]):
        e = e_ref[m]
        ce_ref[m] = nt(sel_ref[...], c_ref[m]).astype(BF)
        ee_ref[m] = nt(sel_ref[...], e).astype(BF)
        picked = nn(perm_ref[...], e).astype(BF)
        lo_ref[m] = picked[:half]
        hi_ref[m] = picked[half:]


def forward_kernel(
    c_ref, e_ref, ch_ref, kl_ref, klt_ref, lf_ref, bf_ref, lh_ref, ll_ref, inc_ref, left_ref, right_ref
):
    rows = c_ref.shape[1]
    lanes = c_ref.shape[2]
    half = left_ref.shape[1]

    @pl.when(pl.program_id(0) == 0)
    def _():
        inc_ref[...] = jnp.zeros_like(inc_ref)

    halo = nn(ch_ref[...], klt_ref[...])
    total = jnp.zeros((rows, lanes), F32)
    for pair in range(c_ref.shape[0] // 2):
        m0 = 2 * pair
        wide = jnp.concatenate([c_ref[m0], c_ref[m0 + 1]], axis=1)
        mixed = nn(kl_ref[...], wide).astype(BF)
        row = []
        for i in range(2):
            y = nn(mixed[:, i * lanes : (i + 1) * lanes], lf_ref[...])
            edge = tn(halo[8 * (m0 + i) : 8 * (m0 + i) + 8].astype(BF), bf_ref[...])
            row.append((y[:, :lanes] + y[:, lanes:] + edge).astype(BF))
        row = jnp.concatenate(row, axis=1)
        loc = nn(lh_ref[...], row) + nn(ll_ref[...], row)
        for i in range(2):
            cut = loc[:, i * lanes : (i + 1) * lanes]
            total = total + e_ref[m0 + i].astype(F32) * cut[:rows]
            left_ref[m0 + i] = cut[rows : rows + half].astype(BF)
            right_ref[m0 + i] = cut[rows + half :].astype(BF)
    inc_ref[...] += total


def obs_kernel(inc_ref, place_ref, q_ref, innov_ref, pulled_ref, edge_ref):
    rows, lanes = inc_ref.shape
    slots = place_ref.shape[1]
    place = place_ref[...]
    r = place // lanes
    c = place - r * lanes
    rt = (lax.broadcasted_iota(jnp.int32, (rows, slots), 0) == r).astype(F32).astype(BF)
    lane_ids = lax.broadcasted_iota(jnp.int32, (lanes, slots), 0)
    hit = lane_ids == c
    inc_t = inc_ref[...].T
    g = jnp.zeros((lanes, slots), F32)
    for part in part3(inc_t):
        g = g + nn(part, rt)
    at_slot = jnp.sum(jnp.where(hit, g, 0.0), axis=0, keepdims=True)
    misfit = q_ref[...] * (at_slot - innov_ref[...])
    e_ids = lax.broadcasted_iota(jnp.int32, (8, slots), 0)
    e_lane = jnp.where(e_ids < 2, e_ids, lanes - 4 + e_ids)
    e_hit = (e_lane == c) & (e_ids < 4)
    pulled = jnp.zeros((rows, lanes), F32)
    edge = jnp.zeros((8, rows), F32)
    for part in part3(misfit):
        part = part.astype(F32)
        pulled = pulled + nt(rt, jnp.where(hit, part, 0.0).astype(BF))
        edge = edge + nt(jnp.where(e_hit, part, 0.0).astype(BF), rt)
    pulled_ref[...] = pulled
    edge_ref[...] = edge


def adjoint_kernel(
    c_ref, e_ref, el_ref, er_ref, elat_ref, p_ref, pl_ref, pr_ref, plat_ref,
    th_ref, tl_ref, xh_ref, xl_ref, la_ref, ba_ref, klt_ref, out_ref,
):
    lanes = c_ref.shape[2]
    count = c_ref.shape[0]
    plat = jnp.concatenate([plat_ref[...]] * count, axis=0)
    plane = (elat_ref[...].astype(F32) * plat).astype(BF)
    halo = nn(plane, xh_ref[...]) + nn(plane, xl_ref[...])
    for pair in range(count // 2):
        m0 = 2 * pair
        ext = []
        for i in range(2):
            ext.append(
                jnp.concatenate(
                    [
                        (e_ref[m0 + i].astype(F32) * p_ref[...]).astype(BF),
                        (el_ref[m0 + i].astype(F32) * pl_ref[...]).astype(BF),
                        (er_ref[m0 + i].astype(F32) * pr_ref[...]).astype(BF),
                    ],
                    axis=0,
                )
            )
        ext = jnp.concatenate(ext, axis=1)
        col = (nn(th_ref[...], ext) + nn(tl_ref[...], ext)).astype(BF)
        spread = []
        for i in range(2):
            y = nn(col[:, i * lanes : (i + 1) * lanes], la_ref[...])
            edge = tn(halo[8 * (m0 + i) : 8 * (m0 + i) + 8].astype(BF), ba_ref[...])
            spread.append((y[:, :lanes] + y[:, lanes:] + edge).astype(BF))
        back = nn(klt_ref[...], jnp.concatenate(spread, axis=1))
        for i in range(2):
            out_ref[m0 + i] = c_ref[m0 + i].astype(F32) + back[:, i * lanes : (i + 1) * lanes]


def full(shape):
    return pl.BlockSpec(shape, lambda g: (0,) * len(shape))


def shift(x, axis, step, wrap):
    n = lax.axis_size(axis)
    if step > 0:
        pairs = [(i, (i + 1) % n) for i in range(n if wrap else n - 1)]
    else:
        pairs = [((i + 1) % n, i) for i in range(n if wrap else n - 1)]
    return lax.ppermute(x, axis, pairs)


def shards(
    control, ensemble, level_mix, lat_taps, lon_taps, obs_location, obs_count, obs_keep, innovation, obs_weight
):
    members, levels, cols, lanes = control.shape
    rows = levels * cols
    half = 2 * levels
    ext = rows + 2 * half
    block = 8 if members % 8 == 0 else 2
    steps = members // block
    c3 = control.reshape(members, rows, lanes)
    e3 = ensemble.reshape(members, rows, lanes)
    params = pltpu.CompilerParams(vmem_limit_bytes=VMEM_LIMIT)

    own = jnp.arange(rows)
    own_level, own_col = own // cols, own % cols
    h = jnp.arange(half)
    ext_level = jnp.concatenate([own_level, h // 2, h // 2])
    ext_col = jnp.concatenate([own_col, h % 2 - 2, cols + h % 2])
    same = ext_level[:, None] == own_level[None, :]
    lon_mat = jnp.where(same, tap_of(own_col[None, :] - ext_col[:, None], lon_taps), 0.0)
    lon_hi, lon_lo = split2(lon_mat)
    lane_id = jnp.arange(lanes)
    edge_pos = jnp.array([-2, -1, lanes, lanes + 1])
    lf_hi, lf_lo = split2(tap_of(lane_id[:, None] - lane_id[None, :], lat_taps))
    lf = jnp.concatenate([lf_hi, lf_lo], axis=1)
    la = jnp.concatenate([lf_hi.T, lf_lo.T], axis=1)
    bf = jnp.concatenate(split2(tap_of(edge_pos[:, None] - lane_id[None, :], lat_taps)), axis=0)
    ba = jnp.concatenate(split2(tap_of(lane_id[None, :] - edge_pos[:, None], lat_taps)), axis=0)
    kl = jnp.where(
        own_col[:, None] == own_col[None, :], jnp.repeat(jnp.repeat(level_mix, cols, 0), cols, 1), 0
    ).astype(BF)
    klt = kl.T
    sel_id = jnp.arange(8)
    sel_lane = jnp.where(sel_id < 2, sel_id, jnp.where(sel_id < 4, lanes - 4 + sel_id, -1))
    sel = (sel_lane[:, None] == lane_id[None, :]).astype(BF)
    pick_level = jnp.concatenate([h // 2, h // 2])
    pick_col = jnp.concatenate([h % 2, cols - 2 + h % 2])
    perm = (pick_level * cols + pick_col)[:, None] == own[None, :]
    perm = perm.astype(BF)

    member_block = lambda a, b: pl.BlockSpec((block, a, b), lambda g: (g, 0, 0))
    ce, ee, low, high = pl.pallas_call(
        edge_kernel,
        grid=(steps,),
        in_specs=[member_block(rows, lanes)] * 2 + [full((8, lanes)), full((2 * half, rows))],
        out_specs=[member_block(8, rows)] * 2 + [member_block(half, lanes)] * 2,
        out_shape=[jax.ShapeDtypeStruct((members, 8, rows), BF)] * 2
        + [jax.ShapeDtypeStruct((members, half, lanes), BF)] * 2,
        compiler_params=params,
        cost_estimate=pl.CostEstimate(flops=10**9, bytes_accessed=13 * 10**6, transcendentals=0),
    )(c3, e3, sel, perm)

    both = jnp.concatenate([ce, ee], axis=0)
    before = shift(both[:, 2:4], "lat", 1, False)
    after = shift(both[:, 0:2], "lat", -1, False)
    lat_halo = jnp.concatenate([before, after], axis=1)
    lat_halo = jnp.concatenate([lat_halo, lat_halo], axis=1)
    ch, eh = lat_halo[:members], lat_halo[members:]
    e_left = shift(high, "lon", 1, True)
    e_right = shift(low, "lon", -1, True)
    corner = nt(eh.reshape(members * 8, rows), perm).astype(BF).reshape(members, 8, 2 * half)
    x_left = shift(corner[:, :4, half:], "lon", 1, True)
    x_right = shift(corner[:, :4, :half], "lon", -1, True)
    x_both = jnp.concatenate([x_left, x_right], axis=2)
    elat = jnp.concatenate([eh, jnp.concatenate([x_both, x_both], axis=1)], axis=2).reshape(members * 8, ext)

    inc, left, right = pl.pallas_call(
        forward_kernel,
        grid=(steps,),
        in_specs=[member_block(rows, lanes)] * 2
        + [pl.BlockSpec((block * 8, rows), lambda g: (g, 0)), full((rows, rows)), full((rows, rows))]
        + [full((lanes, 2 * lanes)), full((8, lanes)), full((ext, rows)), full((ext, rows))],
        out_specs=[full((rows, lanes))] + [member_block(half, lanes)] * 2,
        out_shape=[jax.ShapeDtypeStruct((rows, lanes), F32)]
        + [jax.ShapeDtypeStruct((members, half, lanes), BF)] * 2,
        compiler_params=params,
        cost_estimate=pl.CostEstimate(flops=10**10, bytes_accessed=20 * 10**6, transcendentals=0),
    )(c3, e3, ch.reshape(members * 8, rows), kl, klt, lf, bf, lon_hi, lon_lo)

    places = obs_location[0, 0]
    slots = places.shape[0]
    slot_ids = jnp.arange(slots, dtype=jnp.int32)
    live = (slot_ids < obs_count[0, 0]).astype(F32) * obs_keep[0, 0].astype(F32)
    q = live * obs_weight[0, 0]
    columns = ensemble.reshape(members, -1)[:, places]
    scaled = columns.astype(F32) * jnp.sqrt(q)[None, :]
    local_gram = jnp.dot(scaled, scaled.T, precision=lax.Precision.HIGHEST)
    total_obs = slots * lax.axis_size("lat") * lax.axis_size("lon")
    gram = lax.psum(local_gram, ("lat", "lon"))
    upper = jnp.linalg.cholesky(jnp.eye(members, dtype=F32) + members / total_obs * gram).T

    to_left = jnp.sum(e_left.astype(F32) * left.astype(F32), axis=0)
    to_right = jnp.sum(e_right.astype(F32) * right.astype(F32), axis=0)
    from_right = shift(to_left, "lon", -1, True)
    from_left = shift(to_right, "lon", 1, True)
    cube = inc.reshape(levels, cols, lanes)
    zeros = jnp.zeros((levels, cols - 2, lanes), F32)
    cube = (
        cube
        + jnp.concatenate([from_left.reshape(levels, 2, lanes), zeros], axis=1)
        + jnp.concatenate([zeros, from_right.reshape(levels, 2, lanes)], axis=1)
    )

    pulled, p_edge = pl.pallas_call(
        obs_kernel,
        out_shape=[jax.ShapeDtypeStruct((rows, lanes), F32), jax.ShapeDtypeStruct((8, rows), F32)],
        compiler_params=params,
    )(cube.reshape(rows, lanes), places[None], q[None], innovation[0])

    p_before = shift(p_edge[2:4], "lat", 1, False)
    p_after = shift(p_edge[0:2], "lat", -1, False)
    plat = jnp.concatenate([p_before, p_after], axis=0)
    plat3 = plat.reshape(4, levels, cols)
    p3 = pulled.reshape(levels, cols, lanes)
    p_left = shift(p3[:, cols - 2 :].reshape(half, lanes), "lon", 1, True)
    p_right = shift(p3[:, :2].reshape(half, lanes), "lon", -1, True)
    px_left = shift(plat3[:, :, cols - 2 :].reshape(4, half), "lon", 1, True)
    px_right = shift(plat3[:, :, :2].reshape(4, half), "lon", -1, True)
    plat = jnp.concatenate([plat, px_left, px_right], axis=1)
    plat = jnp.concatenate([plat, plat], axis=0)

    gradient = pl.pallas_call(
        adjoint_kernel,
        grid=(steps,),
        in_specs=[member_block(rows, lanes)] * 2
        + [member_block(half, lanes)] * 2
        + [pl.BlockSpec((block * 8, ext), lambda g: (g, 0))]
        + [full((rows, lanes)), full((half, lanes)), full((half, lanes)), full((8, ext))]
        + [full((rows, ext))] * 2
        + [full((ext, rows))] * 2
        + [full((lanes, 2 * lanes)), full((8, lanes)), full((rows, rows))],
        out_specs=member_block(rows, lanes),
        out_shape=jax.ShapeDtypeStruct((members, rows, lanes), F32),
        compiler_params=params,
        cost_estimate=pl.CostEstimate(flops=10**10, bytes_accessed=24 * 10**6, transcendentals=0),
    )(c3, e3, e_left, e_right, elat, pulled, p_left, p_right, plat,
      lon_hi.T, lon_lo.T, lon_hi, lon_lo, la, ba, klt)
    return gradient.reshape(members, levels, cols, lanes), upper


def solution(mesh):
    in_specs = (
        P(None, None, "lon", "lat"),
        P(None, None, "lon", "lat"),
        P(),
        P(),
        P(),
        P("lon", "lat", None),
        P("lon", "lat"),
        P("lon", "lat", None),
        P("lon", "lat", None),
        P("lon", "lat", None),
    )
    out_specs = (P(None, None, "lon", "lat"), P())
    return jax.shard_map(shards, mesh=mesh, in_specs=in_specs, out_specs=out_specs, check_vma=False)
```

```python
import jax
import jax.numpy as jnp
import numpy as np
from jax import lax
from jax.experimental import pallas as pl
from jax.experimental.pallas import tpu as pltpu
from jax.sharding import PartitionSpec as P

OFFSETS = (-2, -1, 1, 2)
F32, BF = jnp.float32, jnp.bfloat16
VMEM_LIMIT = 56 * 1024 * 1024


def code_of(diff):
    out = np.zeros(diff.shape, np.int32)
    for t, offset in enumerate(OFFSETS):
        out[diff == offset] = t + 1
    out[diff == 0] = 5
    return out


def nn(a, b):
    return jnp.dot(a, b, preferred_element_type=F32)


def nt(a, b):
    return lax.dot_general(a, b, (((1,), (1,)), ((), ())), preferred_element_type=F32)


def tn(a, b):
    return lax.dot_general(a, b, (((0,), (0,)), ((), ())), preferred_element_type=F32)


def part3(x):
    a = x.astype(BF)
    r = x - a.astype(F32)
    b = r.astype(BF)
    c = (r - b.astype(F32)).astype(BF)
    return a, b, c


def setup_kernel(taps_ref, mix_ref, code_ref, codet_ref, ecode_ref, ecodet_ref, spread_ref, same_ref,
                 lf_ref, la_ref, bf_ref, ba_ref, xh_ref, xl_ref, kl_ref, klt_ref, xcode_ref):
    def put(code, base):
        out = jnp.where(code == 5, 1.0, 0.0)
        for t in range(4):
            out = out + jnp.where(code == t + 1, taps_ref[base + t], 0.0)
        hi = out.astype(BF)
        return hi, (out - hi.astype(F32)).astype(BF)

    lf_ref[...] = jnp.concatenate(put(code_ref[...], 0), axis=1)
    la_ref[...] = jnp.concatenate(put(codet_ref[...], 0), axis=1)
    hi, lo = put(ecode_ref[...], 0)
    top = lax.broadcasted_iota(jnp.int32, hi.shape, 0) < 4
    bf_ref[...] = jnp.where(top, hi.astype(F32), lo.astype(F32)).astype(BF)
    hi, lo = put(ecodet_ref[...], 0)
    ba_ref[...] = jnp.where(top, hi.astype(F32), lo.astype(F32)).astype(BF)
    hi, lo = put(xcode_ref[...], 4)
    xh_ref[...] = hi
    xl_ref[...] = lo
    mix = mix_ref[...]
    spread = spread_ref[...]
    same = same_ref[...].astype(F32)
    wide = nn(nn(spread, mix).astype(BF), spread.T)
    kl_ref[...] = (wide * same).astype(BF)
    wide = nn(spread, nt(mix.T, spread).astype(BF))
    klt_ref[...] = (wide * same).astype(BF)


def column_kernel(e_ref, perm_ref, lo_ref, hi_ref):
    half = lo_ref.shape[1]
    lanes = e_ref.shape[2]
    for m in range(0, e_ref.shape[0], 2):
        wide = jnp.concatenate([e_ref[m], e_ref[m + 1]], axis=1)
        picked = nn(perm_ref[...], wide).astype(BF)
        for i in range(2):
            lo_ref[m + i] = picked[:half, i * lanes : (i + 1) * lanes]
            hi_ref[m + i] = picked[half:, i * lanes : (i + 1) * lanes]


def edge_kernel(c_ref, e_ref, sel_ref, ce_ref, ee_ref):
    for m in range(c_ref.shape[0]):
        ce_ref[m] = nt(sel_ref[...], c_ref[m]).astype(BF)
        ee_ref[m] = nt(sel_ref[...], e_ref[m]).astype(BF)


def column_masks(cols, lanes, direction):
    row = lax.broadcasted_iota(jnp.int32, (1, cols, lanes), 1)
    wraps = []
    for offset in OFFSETS:
        o = direction * offset
        wraps.append((row >= cols - o) if o > 0 else (row < -o))
    return row, wraps


def forward_kernel(
    taps_ref, c_ref, e_ref, ch_ref, kl_ref, klt_ref, lf_ref, bf_ref, perm_ref, inc_ref, left_ref, right_ref
):
    rows = c_ref.shape[1]
    lanes = c_ref.shape[2]
    half = left_ref.shape[1]
    levels = half // 2
    cols = rows // levels

    @pl.when(pl.program_id(0) == 0)
    def _():
        inc_ref[...] = jnp.zeros_like(inc_ref)

    _, wraps = column_masks(cols, lanes, 1)
    inner = [jnp.where(w, 0.0, taps_ref[4 + t]) for t, w in enumerate(wraps)]
    outer = [jnp.where(w, taps_ref[4 + t], 0.0) for t, w in enumerate(wraps)]
    halo = nn(ch_ref[...], klt_ref[...])
    total = jnp.zeros((rows, lanes), F32)
    for pair in range(c_ref.shape[0] // 2):
        m0 = 2 * pair
        wide = jnp.concatenate([c_ref[m0], c_ref[m0 + 1]], axis=1)
        mixed = nn(kl_ref[...], wide).astype(BF)
        over = []
        for i in range(2):
            y = nn(mixed[:, i * lanes : (i + 1) * lanes], lf_ref[...])
            edge = tn(halo[8 * (m0 + i) : 8 * (m0 + i) + 8].astype(BF), bf_ref[...])
            row = (y[:, :lanes] + y[:, lanes:] + edge).reshape(levels, cols, lanes)
            loc = row
            out = jnp.zeros_like(row)
            for t in range(4):
                moved = pltpu.roll(row, (-OFFSETS[t]) % cols, 1)
                loc = loc + inner[t] * moved
                out = out + outer[t] * moved
            total = total + e_ref[m0 + i].astype(F32) * loc.reshape(rows, lanes)
            over.append(out.reshape(rows, lanes).astype(BF))
        picked = nn(perm_ref[...], jnp.concatenate(over, axis=1)).astype(BF)
        for i in range(2):
            right_ref[m0 + i] = picked[:half, i * lanes : (i + 1) * lanes]
            left_ref[m0 + i] = picked[half:, i * lanes : (i + 1) * lanes]
    inc_ref[...] += total


def obs_kernel(inc_ref, place_ref, q_ref, innov_ref, pulled_ref, edge_ref):
    rows, lanes = inc_ref.shape
    slots = place_ref.shape[1]
    place = place_ref[...]
    r = place // lanes
    c = place - r * lanes
    rt = (lax.broadcasted_iota(jnp.int32, (rows, slots), 0) == r).astype(F32).astype(BF)
    lane_ids = lax.broadcasted_iota(jnp.int32, (lanes, slots), 0)
    hit = lane_ids == c
    inc_t = inc_ref[...].T
    g = jnp.zeros((lanes, slots), F32)
    for part in part3(inc_t):
        g = g + nn(part, rt)
    at_slot = jnp.sum(jnp.where(hit, g, 0.0), axis=0, keepdims=True)
    misfit = q_ref[...] * (at_slot - innov_ref[...])
    e_ids = lax.broadcasted_iota(jnp.int32, (8, slots), 0)
    e_lane = jnp.where(e_ids < 2, e_ids, lanes - 4 + e_ids)
    e_hit = (e_lane == c) & (e_ids < 4)
    pulled = jnp.zeros((rows, lanes), F32)
    edge = jnp.zeros((8, rows), F32)
    for part in part3(misfit):
        part = part.astype(F32)
        pulled = pulled + nt(rt, jnp.where(hit, part, 0.0).astype(BF))
        edge = edge + nt(jnp.where(e_hit, part, 0.0).astype(BF), rt)
    pulled_ref[...] = pulled
    edge_ref[...] = edge


def adjoint_kernel(
    taps_ref, c_ref, e_ref, el_ref, er_ref, elat_ref, p_ref, pl_ref, pr_ref, plat_ref,
    xh_ref, xl_ref, la_ref, ba_ref, klt_ref, permt_ref, out_ref,
):
    rows = c_ref.shape[1]
    lanes = c_ref.shape[2]
    count = c_ref.shape[0]
    levels = el_ref.shape[1] // 2
    cols = rows // levels
    row_id = lax.broadcasted_iota(jnp.int32, (levels, cols, lanes), 1)
    plat = jnp.concatenate([plat_ref[...]] * count, axis=0)
    plane = (elat_ref[...].astype(F32) * plat).astype(BF)
    halo = nn(plane, xh_ref[...]) + nn(plane, xl_ref[...])
    for pair in range(count // 2):
        m0 = 2 * pair
        side = []
        for i in range(2):
            side.append(
                jnp.concatenate(
                    [
                        (er_ref[m0 + i].astype(F32) * pr_ref[...]).astype(BF),
                        (el_ref[m0 + i].astype(F32) * pl_ref[...]).astype(BF),
                    ],
                    axis=0,
                )
            )
        placed = nn(permt_ref[...], jnp.concatenate(side, axis=1))
        spread = []
        for i in range(2):
            own = (e_ref[m0 + i].astype(F32) * p_ref[...]).astype(BF).astype(F32)
            own = own.reshape(levels, cols, lanes)
            far = placed[:, i * lanes : (i + 1) * lanes].reshape(levels, cols, lanes)
            col = own
            for t in range(4):
                o = OFFSETS[t]
                from_far = (row_id >= cols - o) if o > 0 else (row_id < -o)
                col = col + taps_ref[4 + t] * pltpu.roll(jnp.where(from_far, far, own), o % cols, 1)
            y = nn(col.reshape(rows, lanes).astype(BF), la_ref[...])
            edge = tn(halo[8 * (m0 + i) : 8 * (m0 + i) + 8].astype(BF), ba_ref[...])
            spread.append((y[:, :lanes] + y[:, lanes:] + edge).astype(BF))
        back = nn(klt_ref[...], jnp.concatenate(spread, axis=1))
        for i in range(2):
            out_ref[m0 + i] = c_ref[m0 + i].astype(F32) + back[:, i * lanes : (i + 1) * lanes]


def full(shape):
    return pl.BlockSpec(shape, lambda g: (0,) * len(shape))


def shift(x, axis, step, wrap):
    n = lax.axis_size(axis)
    if step > 0:
        pairs = [(i, (i + 1) % n) for i in range(n if wrap else n - 1)]
    else:
        pairs = [((i + 1) % n, i) for i in range(n if wrap else n - 1)]
    return lax.ppermute(x, axis, pairs)


def shards(
    control, ensemble, level_mix, lat_taps, lon_taps, obs_location, obs_count, obs_keep, innovation, obs_weight
):
    members, levels, cols, lanes = control.shape
    rows = levels * cols
    half = 2 * levels
    ext = rows + 2 * half
    block = 8 if members % 8 == 0 else 2
    steps = members // block
    c3 = control.reshape(members, rows, lanes)
    e3 = ensemble.reshape(members, rows, lanes)
    params = pltpu.CompilerParams(vmem_limit_bytes=VMEM_LIMIT)

    smem = pl.BlockSpec(memory_space=pltpu.SMEM)
    own = np.arange(rows)
    own_level, own_col = own // cols, own % cols
    h = np.arange(half)
    ext_level = np.concatenate([own_level, h // 2, h // 2])
    ext_col = np.concatenate([own_col, h % 2 - 2, cols + h % 2])
    same_level = ext_level[:, None] == own_level[None, :]
    xcode = np.where(same_level, code_of(own_col[None, :] - ext_col[:, None]), 0).astype(np.int32)
    lane_id = np.arange(lanes)
    lat_code = code_of(lane_id[:, None] - lane_id[None, :])
    edge_pos = np.array([-2, -1, lanes, lanes + 1] * 2)
    e_code = code_of(edge_pos[:, None] - lane_id[None, :])
    e_code_t = code_of(lane_id[None, :] - edge_pos[:, None])
    spread_levels = (own_level[:, None] == np.arange(levels)[None, :]).astype(np.float32)
    same_col = (own_col[:, None] == own_col[None, :]).astype(np.float32)
    sel_lane = np.array([0, 1, lanes - 2, lanes - 1, -1, -1, -1, -1])
    sel = jnp.asarray((sel_lane[:, None] == lane_id[None, :]).astype(np.float32).astype(BF))
    pick_level = np.concatenate([h // 2, h // 2])
    pick_col = np.concatenate([h % 2, cols - 2 + h % 2])
    perm_np = ((pick_level * cols + pick_col)[:, None] == own[None, :]).astype(np.float32)
    perm = jnp.asarray(perm_np.astype(BF))
    perm_t = jnp.asarray(perm_np.T.astype(BF))
    taps = jnp.concatenate([lat_taps, lon_taps])

    member_block = lambda a, b: pl.BlockSpec((block, a, b), lambda g: (g, 0, 0))
    low, high = pl.pallas_call(
        column_kernel,
        grid=(steps,),
        in_specs=[member_block(rows, lanes), full((2 * half, rows))],
        out_specs=[member_block(half, lanes)] * 2,
        out_shape=[jax.ShapeDtypeStruct((members, half, lanes), BF)] * 2,
        compiler_params=params,
        cost_estimate=pl.CostEstimate(flops=10**9, bytes_accessed=8 * 10**6, transcendentals=0),
    )(e3, perm)
    e_left = shift(high, "lon", 1, True)
    e_right = shift(low, "lon", -1, True)

    ce, ee = pl.pallas_call(
        edge_kernel,
        grid=(steps,),
        in_specs=[member_block(rows, lanes)] * 2 + [full((8, lanes))],
        out_specs=[member_block(8, rows)] * 2,
        out_shape=[jax.ShapeDtypeStruct((members, 8, rows), BF)] * 2,
        compiler_params=params,
        cost_estimate=pl.CostEstimate(flops=10**9, bytes_accessed=11 * 10**6, transcendentals=0),
    )(c3, e3, sel)
    vm = pl.BlockSpec(memory_space=pltpu.VMEM)
    lf, la, bf, ba, lon_hi, lon_lo, kl, klt = pl.pallas_call(
        lambda *refs: setup_kernel(*refs[:8], *refs[9:], refs[8]),
        in_specs=[smem] + [vm] * 8,
        out_specs=[vm] * 8,
        out_shape=[jax.ShapeDtypeStruct(shape, BF) for shape in (
            (lanes, 2 * lanes), (lanes, 2 * lanes), (8, lanes), (8, lanes),
            (ext, rows), (ext, rows), (rows, rows), (rows, rows))],
        compiler_params=params,
        name="setup",
    )(taps, level_mix, jnp.asarray(lat_code), jnp.asarray(lat_code.T.copy()), jnp.asarray(e_code),
      jnp.asarray(e_code_t), jnp.asarray(spread_levels.astype(BF)), jnp.asarray(same_col.astype(BF)),
      jnp.asarray(xcode))

    both = jnp.concatenate([ce, ee], axis=0)
    before = shift(both[:, 2:4], "lat", 1, False)
    after = shift(both[:, 0:2], "lat", -1, False)
    lat_halo = jnp.concatenate([before, after], axis=1)
    lat_halo = jnp.concatenate([lat_halo, lat_halo], axis=1)
    ch, eh = lat_halo[:members], lat_halo[members:]
    corner = nt(eh.reshape(members * 8, rows), perm).astype(BF).reshape(members, 8, 2 * half)
    x_left = shift(corner[:, :4, half:], "lon", 1, True)
    x_right = shift(corner[:, :4, :half], "lon", -1, True)
    x_both = jnp.concatenate([x_left, x_right], axis=2)
    elat = jnp.concatenate([eh, jnp.concatenate([x_both, x_both], axis=1)], axis=2).reshape(members * 8, ext)

    inc, left, right = pl.pallas_call(
        forward_kernel,
        grid=(steps,),
        in_specs=[smem]
        + [member_block(rows, lanes)] * 2
        + [pl.BlockSpec((block * 8, rows), lambda g: (g, 0)), full((rows, rows)), full((rows, rows))]
        + [full((lanes, 2 * lanes)), full((8, lanes)), full((2 * half, rows))],
        out_specs=[full((rows, lanes))] + [member_block(half, lanes)] * 2,
        out_shape=[jax.ShapeDtypeStruct((rows, lanes), F32)]
        + [jax.ShapeDtypeStruct((members, half, lanes), BF)] * 2,
        compiler_params=params,
        cost_estimate=pl.CostEstimate(flops=10**10, bytes_accessed=20 * 10**6, transcendentals=0),
    )(taps, c3, e3, ch.reshape(members * 8, rows), kl, klt, lf, bf, perm)

    places = obs_location[0, 0]
    slots = places.shape[0]
    slot_ids = jnp.arange(slots, dtype=jnp.int32)
    live = (slot_ids < obs_count[0, 0]).astype(F32) * obs_keep[0, 0].astype(F32)
    q = live * obs_weight[0, 0]
    columns = ensemble.reshape(members, -1)[:, places]
    scaled = columns.astype(F32) * jnp.sqrt(q)[None, :]
    local_gram = jnp.dot(scaled, scaled.T, precision=lax.Precision.HIGHEST)
    local_gram, inc, left, right = lax.optimization_barrier((local_gram, inc, left, right))
    total_obs = slots * lax.axis_size("lat") * lax.axis_size("lon")
    gram = lax.psum(local_gram, ("lat", "lon"))
    upper = jnp.linalg.cholesky(jnp.eye(members, dtype=F32) + members / total_obs * gram).T

    to_left = jnp.sum(e_left.astype(F32) * left.astype(F32), axis=0)
    to_right = jnp.sum(e_right.astype(F32) * right.astype(F32), axis=0)
    from_right = shift(to_left, "lon", -1, True)
    from_left = shift(to_right, "lon", 1, True)
    cube = inc.reshape(levels, cols, lanes)
    zeros = jnp.zeros((levels, cols - 2, lanes), F32)
    cube = (
        cube
        + jnp.concatenate([from_left.reshape(levels, 2, lanes), zeros], axis=1)
        + jnp.concatenate([zeros, from_right.reshape(levels, 2, lanes)], axis=1)
    )

    pulled, p_edge = pl.pallas_call(
        obs_kernel,
        out_shape=[jax.ShapeDtypeStruct((rows, lanes), F32), jax.ShapeDtypeStruct((8, rows), F32)],
        compiler_params=params,
    )(cube.reshape(rows, lanes), places[None], q[None], innovation[0])

    p_before = shift(p_edge[2:4], "lat", 1, False)
    p_after = shift(p_edge[0:2], "lat", -1, False)
    plat = jnp.concatenate([p_before, p_after], axis=0)
    plat3 = plat.reshape(4, levels, cols)
    p3 = pulled.reshape(levels, cols, lanes)
    def packed(piece, corner):
        wide = jnp.pad(corner.reshape(4, half), ((0, 4), (0, lanes - half)))
        return jnp.concatenate([piece.reshape(half, lanes), wide], axis=0)

    p_left = shift(packed(p3[:, cols - 2 :], plat3[:, :, cols - 2 :]), "lon", 1, True)
    p_right = shift(packed(p3[:, :2], plat3[:, :, :2]), "lon", -1, True)
    px_left, px_right = p_left[half : half + 4, :half], p_right[half : half + 4, :half]
    p_left, p_right = p_left[:half], p_right[:half]
    plat = jnp.concatenate([plat, px_left, px_right], axis=1)
    plat = jnp.concatenate([plat, plat], axis=0)

    gradient = pl.pallas_call(
        adjoint_kernel,
        grid=(steps,),
        in_specs=[smem]
        + [member_block(rows, lanes)] * 2
        + [member_block(half, lanes)] * 2
        + [pl.BlockSpec((block * 8, ext), lambda g: (g, 0))]
        + [full((rows, lanes)), full((half, lanes)), full((half, lanes)), full((8, ext))]
        + [full((ext, rows))] * 2
        + [full((lanes, 2 * lanes)), full((8, lanes)), full((rows, rows)), full((rows, 2 * half))],
        out_specs=member_block(rows, lanes),
        out_shape=jax.ShapeDtypeStruct((members, rows, lanes), F32),
        compiler_params=params,
        cost_estimate=pl.CostEstimate(flops=10**10, bytes_accessed=24 * 10**6, transcendentals=0),
    )(taps, c3, e3, e_left, e_right, elat, pulled, p_left, p_right, plat,
      lon_hi, lon_lo, la, ba, klt, perm_t)
    return gradient.reshape(members, levels, cols, lanes), upper


def solution(mesh):
    in_specs = (
        P(None, None, "lon", "lat"),
        P(None, None, "lon", "lat"),
        P(),
        P(),
        P(),
        P("lon", "lat", None),
        P("lon", "lat"),
        P("lon", "lat", None),
        P("lon", "lat", None),
        P("lon", "lat", None),
    )
    out_specs = (P(None, None, "lon", "lat"), P())
    return jax.shard_map(shards, mesh=mesh, in_specs=in_specs, out_specs=out_specs, check_vma=False)
```

```python
import jax
import jax.numpy as jnp
import numpy as np
from jax import lax
from jax.experimental import pallas as pl
from jax.experimental.pallas import tpu as pltpu
from jax.sharding import PartitionSpec as P

OFFSETS = (-2, -1, 1, 2)
F32, BF = jnp.float32, jnp.bfloat16
VMEM_LIMIT = 56 * 1024 * 1024


def code_of(diff):
    out = np.zeros(diff.shape, np.int32)
    for t, offset in enumerate(OFFSETS):
        out[diff == offset] = t + 1
    out[diff == 0] = 5
    return out


def nn(a, b):
    return jnp.dot(a, b, preferred_element_type=F32)


def nt(a, b):
    return lax.dot_general(a, b, (((1,), (1,)), ((), ())), preferred_element_type=F32)


def tn(a, b):
    return lax.dot_general(a, b, (((0,), (0,)), ((), ())), preferred_element_type=F32)


def part3(x):
    a = x.astype(BF)
    r = x - a.astype(F32)
    b = r.astype(BF)
    c = (r - b.astype(F32)).astype(BF)
    return a, b, c


def setup_kernel(taps_ref, mix_ref, code_ref, codet_ref, ecode_ref, ecodet_ref, spread_ref, same_ref,
                 lf_ref, la_ref, bf_ref, ba_ref, xh_ref, xl_ref, kl_ref, klt_ref, xcode_ref):
    def put(code, base):
        out = jnp.where(code == 5, 1.0, 0.0)
        for t in range(4):
            out = out + jnp.where(code == t + 1, taps_ref[base + t], 0.0)
        hi = out.astype(BF)
        return hi, (out - hi.astype(F32)).astype(BF)

    lf_ref[...] = jnp.concatenate(put(code_ref[...], 0), axis=1)
    la_ref[...] = jnp.concatenate(put(codet_ref[...], 0), axis=1)
    hi, lo = put(ecode_ref[...], 0)
    top = lax.broadcasted_iota(jnp.int32, hi.shape, 0) < 4
    bf_ref[...] = jnp.where(top, hi.astype(F32), lo.astype(F32)).astype(BF)
    hi, lo = put(ecodet_ref[...], 0)
    ba_ref[...] = jnp.where(top, hi.astype(F32), lo.astype(F32)).astype(BF)
    hi, lo = put(xcode_ref[...], 4)
    xh_ref[...] = hi
    xl_ref[...] = lo
    mix = mix_ref[...]
    spread = spread_ref[...]
    same = same_ref[...].astype(F32)
    wide = nn(nn(spread, mix).astype(BF), spread.T)
    kl_ref[...] = (wide * same).astype(BF)
    wide = nn(spread, nt(mix.T, spread).astype(BF))
    klt_ref[...] = (wide * same).astype(BF)


def column_kernel(e_ref, perm_ref, lo_ref, hi_ref):
    half = lo_ref.shape[1]
    lanes = e_ref.shape[2]
    for m in range(0, e_ref.shape[0], 2):
        wide = jnp.concatenate([e_ref[m], e_ref[m + 1]], axis=1)
        picked = nn(perm_ref[...], wide).astype(BF)
        for i in range(2):
            lo_ref[m + i] = picked[:half, i * lanes : (i + 1) * lanes]
            hi_ref[m + i] = picked[half:, i * lanes : (i + 1) * lanes]


def edge_kernel(c_ref, e_ref, sel_ref, ce_ref, ee_ref):
    for m in range(c_ref.shape[0]):
        ce_ref[m] = nt(sel_ref[...], c_ref[m]).astype(BF)
        ee_ref[m] = nt(sel_ref[...], e_ref[m]).astype(BF)


def column_masks(cols, lanes, direction):
    row = lax.broadcasted_iota(jnp.int32, (1, cols, lanes), 1)
    wraps = []
    for offset in OFFSETS:
        o = direction * offset
        wraps.append((row >= cols - o) if o > 0 else (row < -o))
    return row, wraps


def forward_kernel(
    taps_ref, c_ref, e_ref, ch_ref, kl_ref, klt_ref, lf_ref, bf_ref, perm_ref, inc_ref, left_ref, right_ref
):
    rows = c_ref.shape[1]
    lanes = c_ref.shape[2]
    half = left_ref.shape[1]
    levels = half // 2
    cols = rows // levels

    @pl.when(pl.program_id(0) == 0)
    def _():
        inc_ref[...] = jnp.zeros_like(inc_ref)

    _, wraps = column_masks(cols, lanes, 1)
    inner = [jnp.where(w, 0.0, taps_ref[4 + t]) for t, w in enumerate(wraps)]
    outer = [jnp.where(w, taps_ref[4 + t], 0.0) for t, w in enumerate(wraps)]
    halo = nn(ch_ref[...], klt_ref[...])
    total = jnp.zeros((rows, lanes), F32)
    for pair in range(c_ref.shape[0] // 2):
        m0 = 2 * pair
        wide = jnp.concatenate([c_ref[m0], c_ref[m0 + 1]], axis=1)
        mixed = nn(kl_ref[...], wide).astype(BF)
        over = []
        for i in range(2):
            y = nn(mixed[:, i * lanes : (i + 1) * lanes], lf_ref[...])
            edge = tn(halo[8 * (m0 + i) : 8 * (m0 + i) + 8].astype(BF), bf_ref[...])
            row = (y[:, :lanes] + y[:, lanes:] + edge).reshape(levels, cols, lanes)
            loc = row
            out = jnp.zeros_like(row)
            for t in range(4):
                moved = pltpu.roll(row, (-OFFSETS[t]) % cols, 1)
                loc = loc + inner[t] * moved
                out = out + outer[t] * moved
            total = total + e_ref[m0 + i].astype(F32) * loc.reshape(rows, lanes)
            over.append(out.reshape(rows, lanes).astype(BF))
        picked = nn(perm_ref[...], jnp.concatenate(over, axis=1)).astype(BF)
        for i in range(2):
            right_ref[m0 + i] = picked[:half, i * lanes : (i + 1) * lanes]
            left_ref[m0 + i] = picked[half:, i * lanes : (i + 1) * lanes]
    inc_ref[...] += total


def obs_kernel(inc_ref, place_ref, q_ref, innov_ref, pulled_ref, edge_ref):
    rows, lanes = inc_ref.shape
    slots = place_ref.shape[1]
    place = place_ref[...]
    r = place // lanes
    c = place - r * lanes
    rt = (lax.broadcasted_iota(jnp.int32, (rows, slots), 0) == r).astype(F32).astype(BF)
    lane_ids = lax.broadcasted_iota(jnp.int32, (lanes, slots), 0)
    hit = lane_ids == c
    inc_t = inc_ref[...].T
    g = jnp.zeros((lanes, slots), F32)
    for part in part3(inc_t):
        g = g + nn(part, rt)
    at_slot = jnp.sum(jnp.where(hit, g, 0.0), axis=0, keepdims=True)
    misfit = q_ref[...] * (at_slot - innov_ref[...])
    e_ids = lax.broadcasted_iota(jnp.int32, (8, slots), 0)
    e_lane = jnp.where(e_ids < 2, e_ids, lanes - 4 + e_ids)
    e_hit = (e_lane == c) & (e_ids < 4)
    pulled = jnp.zeros((rows, lanes), F32)
    edge = jnp.zeros((8, rows), F32)
    for part in part3(misfit):
        part = part.astype(F32)
        pulled = pulled + nt(rt, jnp.where(hit, part, 0.0).astype(BF))
        edge = edge + nt(jnp.where(e_hit, part, 0.0).astype(BF), rt)
    pulled_ref[...] = pulled
    edge_ref[...] = edge


def adjoint_kernel(
    taps_ref, c_ref, e_ref, el_ref, er_ref, elat_ref, p_ref, pl_ref, pr_ref, plat_ref,
    xh_ref, xl_ref, la_ref, ba_ref, klt_ref, permt_ref, out_ref,
):
    rows = c_ref.shape[1]
    lanes = c_ref.shape[2]
    count = c_ref.shape[0]
    levels = el_ref.shape[1] // 2
    cols = rows // levels
    row_id = lax.broadcasted_iota(jnp.int32, (levels, cols, lanes), 1)
    plat = jnp.concatenate([plat_ref[...]] * count, axis=0)
    plane = (elat_ref[...].astype(F32) * plat).astype(BF)
    halo = nn(plane, xh_ref[...]) + nn(plane, xl_ref[...])
    for pair in range(count // 2):
        m0 = 2 * pair
        side = []
        for i in range(2):
            side.append(
                jnp.concatenate(
                    [
                        (er_ref[m0 + i].astype(F32) * pr_ref[...]).astype(BF),
                        (el_ref[m0 + i].astype(F32) * pl_ref[...]).astype(BF),
                    ],
                    axis=0,
                )
            )
        placed = nn(permt_ref[...], jnp.concatenate(side, axis=1))
        spread = []
        for i in range(2):
            own = (e_ref[m0 + i].astype(F32) * p_ref[...]).astype(BF).astype(F32)
            own = own.reshape(levels, cols, lanes)
            far = placed[:, i * lanes : (i + 1) * lanes].reshape(levels, cols, lanes)
            col = own
            for t in range(4):
                o = OFFSETS[t]
                from_far = (row_id >= cols - o) if o > 0 else (row_id < -o)
                col = col + taps_ref[4 + t] * pltpu.roll(jnp.where(from_far, far, own), o % cols, 1)
            y = nn(col.reshape(rows, lanes).astype(BF), la_ref[...])
            edge = tn(halo[8 * (m0 + i) : 8 * (m0 + i) + 8].astype(BF), ba_ref[...])
            spread.append((y[:, :lanes] + y[:, lanes:] + edge).astype(BF))
        back = nn(klt_ref[...], jnp.concatenate(spread, axis=1))
        for i in range(2):
            out_ref[m0 + i] = c_ref[m0 + i].astype(F32) + back[:, i * lanes : (i + 1) * lanes]


def full(shape):
    return pl.BlockSpec(shape, lambda g: (0,) * len(shape))


def shift(x, axis, step, wrap):
    n = lax.axis_size(axis)
    if step > 0:
        pairs = [(i, (i + 1) % n) for i in range(n if wrap else n - 1)]
    else:
        pairs = [((i + 1) % n, i) for i in range(n if wrap else n - 1)]
    return lax.ppermute(x, axis, pairs)


def butterfly(x, axis):
    n = lax.axis_size(axis)
    if n & (n - 1):
        return lax.psum(x, axis)
    bit = 1
    while bit < n:
        x = x + lax.ppermute(x, axis, [(i, i ^ bit) for i in range(n)])
        bit *= 2
    return x


def shards(
    control, ensemble, level_mix, lat_taps, lon_taps, obs_location, obs_count, obs_keep, innovation, obs_weight
):
    members, levels, cols, lanes = control.shape
    rows = levels * cols
    half = 2 * levels
    ext = rows + 2 * half
    block = 8 if members % 8 == 0 else 2
    steps = members // block
    c3 = control.reshape(members, rows, lanes)
    e3 = ensemble.reshape(members, rows, lanes)
    params = pltpu.CompilerParams(vmem_limit_bytes=VMEM_LIMIT)

    smem = pl.BlockSpec(memory_space=pltpu.SMEM)
    own = np.arange(rows)
    own_level, own_col = own // cols, own % cols
    h = np.arange(half)
    ext_level = np.concatenate([own_level, h // 2, h // 2])
    ext_col = np.concatenate([own_col, h % 2 - 2, cols + h % 2])
    same_level = ext_level[:, None] == own_level[None, :]
    xcode = np.where(same_level, code_of(own_col[None, :] - ext_col[:, None]), 0).astype(np.int32)
    lane_id = np.arange(lanes)
    lat_code = code_of(lane_id[:, None] - lane_id[None, :])
    edge_pos = np.array([-2, -1, lanes, lanes + 1] * 2)
    e_code = code_of(edge_pos[:, None] - lane_id[None, :])
    e_code_t = code_of(lane_id[None, :] - edge_pos[:, None])
    spread_levels = (own_level[:, None] == np.arange(levels)[None, :]).astype(np.float32)
    same_col = (own_col[:, None] == own_col[None, :]).astype(np.float32)
    sel_lane = np.array([0, 1, lanes - 2, lanes - 1, -1, -1, -1, -1])
    sel = jnp.asarray((sel_lane[:, None] == lane_id[None, :]).astype(np.float32).astype(BF))
    pick_level = np.concatenate([h // 2, h // 2])
    pick_col = np.concatenate([h % 2, cols - 2 + h % 2])
    perm_np = ((pick_level * cols + pick_col)[:, None] == own[None, :]).astype(np.float32)
    perm = jnp.asarray(perm_np.astype(BF))
    perm_t = jnp.asarray(perm_np.T.astype(BF))
    taps = jnp.concatenate([lat_taps, lon_taps])

    member_block = lambda a, b: pl.BlockSpec((block, a, b), lambda g: (g, 0, 0))
    low, high = pl.pallas_call(
        column_kernel,
        grid=(steps,),
        in_specs=[member_block(rows, lanes), full((2 * half, rows))],
        out_specs=[member_block(half, lanes)] * 2,
        out_shape=[jax.ShapeDtypeStruct((members, half, lanes), BF)] * 2,
        compiler_params=params,
        cost_estimate=pl.CostEstimate(flops=10**9, bytes_accessed=8 * 10**6, transcendentals=0),
    )(e3, perm)

    sel, e_left_src, e_right_src = lax.optimization_barrier((sel, high, low))
    e_left = shift(e_left_src, "lon", 1, True)
    e_right = shift(e_right_src, "lon", -1, True)
    ce, ee = pl.pallas_call(
        edge_kernel,
        grid=(steps,),
        in_specs=[member_block(rows, lanes)] * 2 + [full((8, lanes))],
        out_specs=[member_block(8, rows)] * 2,
        out_shape=[jax.ShapeDtypeStruct((members, 8, rows), BF)] * 2,
        compiler_params=params,
        cost_estimate=pl.CostEstimate(flops=10**9, bytes_accessed=11 * 10**6, transcendentals=0),
    )(c3, e3, sel)
    vm = pl.BlockSpec(memory_space=pltpu.VMEM)
    lf, la, bf, ba, lon_hi, lon_lo, kl, klt = pl.pallas_call(
        lambda *refs: setup_kernel(*refs[:8], *refs[9:], refs[8]),
        in_specs=[smem] + [vm] * 8,
        out_specs=[vm] * 8,
        out_shape=[jax.ShapeDtypeStruct(shape, BF) for shape in (
            (lanes, 2 * lanes), (lanes, 2 * lanes), (8, lanes), (8, lanes),
            (ext, rows), (ext, rows), (rows, rows), (rows, rows))],
        compiler_params=params,
        name="setup",
    )(taps, level_mix, jnp.asarray(lat_code), jnp.asarray(lat_code.T.copy()), jnp.asarray(e_code),
      jnp.asarray(e_code_t), jnp.asarray(spread_levels.astype(BF)), jnp.asarray(same_col.astype(BF)),
      jnp.asarray(xcode))

    both = jnp.concatenate([ce, ee], axis=0)
    before = shift(both[:, 2:4], "lat", 1, False)
    after = shift(both[:, 0:2], "lat", -1, False)
    lat_halo = jnp.concatenate([before, after], axis=1)
    lat_halo = jnp.concatenate([lat_halo, lat_halo], axis=1)
    ch, eh = lat_halo[:members], lat_halo[members:]
    corner = nt(eh.reshape(members * 8, rows), perm).astype(BF).reshape(members, 8, 2 * half)
    x_left = shift(corner[:, :4, half:], "lon", 1, True)
    x_right = shift(corner[:, :4, :half], "lon", -1, True)
    x_both = jnp.concatenate([x_left, x_right], axis=2)
    elat = jnp.concatenate([eh, jnp.concatenate([x_both, x_both], axis=1)], axis=2).reshape(members * 8, ext)

    inc, left, right = pl.pallas_call(
        forward_kernel,
        grid=(steps,),
        in_specs=[smem]
        + [member_block(rows, lanes)] * 2
        + [pl.BlockSpec((block * 8, rows), lambda g: (g, 0)), full((rows, rows)), full((rows, rows))]
        + [full((lanes, 2 * lanes)), full((8, lanes)), full((2 * half, rows))],
        out_specs=[full((rows, lanes))] + [member_block(half, lanes)] * 2,
        out_shape=[jax.ShapeDtypeStruct((rows, lanes), F32)]
        + [jax.ShapeDtypeStruct((members, half, lanes), BF)] * 2,
        compiler_params=params,
        cost_estimate=pl.CostEstimate(flops=10**10, bytes_accessed=20 * 10**6, transcendentals=0),
    )(taps, c3, e3, ch.reshape(members * 8, rows), kl, klt, lf, bf, perm)

    places = obs_location[0, 0]
    slots = places.shape[0]
    slot_ids = jnp.arange(slots, dtype=jnp.int32)
    live = (slot_ids < obs_count[0, 0]).astype(F32) * obs_keep[0, 0].astype(F32)
    q = live * obs_weight[0, 0]
    columns = ensemble.reshape(members, -1)[:, places]
    scaled = columns.astype(F32) * jnp.sqrt(q)[None, :]
    local_gram = jnp.dot(scaled, scaled.T, precision=lax.Precision.HIGHEST)
    total_obs = slots * lax.axis_size("lat") * lax.axis_size("lon")
    gram = butterfly(butterfly(local_gram, "lat"), "lon")
    upper = jnp.linalg.cholesky(jnp.eye(members, dtype=F32) + members / total_obs * gram).T

    to_left = jnp.sum(e_left.astype(F32) * left.astype(F32), axis=0)
    to_right = jnp.sum(e_right.astype(F32) * right.astype(F32), axis=0)
    from_right = shift(to_left, "lon", -1, True)
    from_left = shift(to_right, "lon", 1, True)
    cube = inc.reshape(levels, cols, lanes)
    zeros = jnp.zeros((levels, cols - 2, lanes), F32)
    cube = (
        cube
        + jnp.concatenate([from_left.reshape(levels, 2, lanes), zeros], axis=1)
        + jnp.concatenate([zeros, from_right.reshape(levels, 2, lanes)], axis=1)
    )

    pulled, p_edge = pl.pallas_call(
        obs_kernel,
        out_shape=[jax.ShapeDtypeStruct((rows, lanes), F32), jax.ShapeDtypeStruct((8, rows), F32)],
        compiler_params=params,
    )(cube.reshape(rows, lanes), places[None], q[None], innovation[0])

    p_before = shift(p_edge[2:4], "lat", 1, False)
    p_after = shift(p_edge[0:2], "lat", -1, False)
    plat = jnp.concatenate([p_before, p_after], axis=0)
    plat3 = plat.reshape(4, levels, cols)
    p3 = pulled.reshape(levels, cols, lanes)
    def packed(piece, corner):
        wide = jnp.pad(corner.reshape(4, half), ((0, 4), (0, lanes - half)))
        return jnp.concatenate([piece.reshape(half, lanes), wide], axis=0)

    p_left = shift(packed(p3[:, cols - 2 :], plat3[:, :, cols - 2 :]), "lon", 1, True)
    p_right = shift(packed(p3[:, :2], plat3[:, :, :2]), "lon", -1, True)
    px_left, px_right = p_left[half : half + 4, :half], p_right[half : half + 4, :half]
    p_left, p_right = p_left[:half], p_right[:half]
    plat = jnp.concatenate([plat, px_left, px_right], axis=1)
    plat = jnp.concatenate([plat, plat], axis=0)

    gradient = pl.pallas_call(
        adjoint_kernel,
        grid=(steps,),
        in_specs=[smem]
        + [member_block(rows, lanes)] * 2
        + [member_block(half, lanes)] * 2
        + [pl.BlockSpec((block * 8, ext), lambda g: (g, 0))]
        + [full((rows, lanes)), full((half, lanes)), full((half, lanes)), full((8, ext))]
        + [full((ext, rows))] * 2
        + [full((lanes, 2 * lanes)), full((8, lanes)), full((rows, rows)), full((rows, 2 * half))],
        out_specs=member_block(rows, lanes),
        out_shape=jax.ShapeDtypeStruct((members, rows, lanes), F32),
        compiler_params=params,
        cost_estimate=pl.CostEstimate(flops=10**10, bytes_accessed=24 * 10**6, transcendentals=0),
    )(taps, c3, e3, e_left, e_right, elat, pulled, p_left, p_right, plat,
      lon_hi, lon_lo, la, ba, klt, perm_t)
    return gradient.reshape(members, levels, cols, lanes), upper


def solution(mesh):
    in_specs = (
        P(None, None, "lon", "lat"),
        P(None, None, "lon", "lat"),
        P(),
        P(),
        P(),
        P("lon", "lat", None),
        P("lon", "lat"),
        P("lon", "lat", None),
        P("lon", "lat", None),
        P("lon", "lat", None),
    )
    out_specs = (P(None, None, "lon", "lat"), P())
    return jax.shard_map(shards, mesh=mesh, in_specs=in_specs, out_specs=out_specs, check_vma=False)
```
